32 devices in a mesh: week: 4 (over x, core), row: 4 (over z), col: 2 (over y).
Axes of the slice: x: 2, y: 2, z: 4, core: 2. Of those that a mesh axis runs over, the one named last changes fastest.
Arguments:
- sensitivity: bfloat16 [4, 3, 1024, 4096], P('week', None, None, ('row', 'col')), may hold values from -0.1875 to 0.1875
- reach: int32 [4, 1024], P('week'), may hold values from 0 to 2, as said below
- obs_weight: float32 [4, 1024], P('week'), may hold values from 0.25 to 4
- prior_precision: float32 [4, 4096], P('week', ('row', 'col')), may hold values from 0.5 to 4
- pivot_solve: bfloat16 [4096, 4096], P('week', ('row', 'col')), may hold values from -0.09375 to 0.09375
Outputs:
- hessian_band: float32 [4, 3, 4096, 4096], P('week', None, ('row', 'col'))
- panel: bfloat16 [4096, 4096], P(('row', 'col'), 'week')
- schur: float32 [4096, 4096], P(('row', 'col'), 'week')
The draws below stay inside these ranges and needn't reach their ends.
Inputs may be any that keep to these rules, and one draw needn't show every extreme that they name: The number of observations at each reach differs widely from week to week; in some week w >= 2 every observation has reach 2.
All inputs are finite; a program needn't handle non-finite values.
Results may differ from the reference program's by a relative error of at most 0.013.
Values may be sent and summed in bfloat16 or wider, within the bound.
A program may use at most 128 MiB of HBM per device.

```python
import math
import jax
import jax.numpy as jnp

REG = 4096
OBS = 1024
LAGS = 3
NW = 4
N_WEEK = 4


def draw_reach(key, part):
    base = jax.random.fold_in(key, 7)
    keys = jax.random.split(base, 7)
    heavy = LAGS - 1 + jax.random.randint(keys[0], (), 0, NW - LAGS + 1)
    light = jnp.where(heavy + 1 < NW, heavy + 1, heavy - 1)
    lower = jax.random.randint(keys[1], (NW, 1), 0, 1001)
    spread = jax.random.randint(keys[2], (NW, 1), 0, 1001)
    upper = jnp.minimum(lower + spread, 1000)
    unit = jax.random.randint(keys[3], (NW, OBS), 0, 1000)
    mixed = jnp.minimum((unit >= lower).astype(jnp.int32) + (unit >= upper).astype(jnp.int32), LAGS - 1)
    count = jax.random.randint(keys[4], (), 1, OBS // 8 + 1)
    order = jax.random.permutation(keys[5], OBS)
    low_reach = jax.random.randint(keys[6], (OBS,), 0, LAGS - 1)
    light_row = jnp.where(order < count, LAGS - 1, low_reach)
    weeks = jnp.arange(NW)[:, None]
    result = jnp.where(weeks == heavy, LAGS - 1, jnp.where(weeks == light, light_row[None, :], mixed))
    return result.astype(jnp.int32)


def block_scale(rng, dims, pieces, least, largest):
    factor_of = 1.0
    for axis_at, shards_of in pieces:
        steps = jax.random.uniform(jax.random.fold_in(jax.random.fold_in(rng, 6), axis_at), (shards_of,), jnp.float32, least / len(pieces), largest / len(pieces))
        factor_of = factor_of * jnp.repeat(jnp.exp(steps), dims[axis_at] // shards_of).reshape((-1,) + (1,) * (len(dims) - 1 - axis_at))
    return factor_of


def centred(key, shape, deviation, limit, shards=(), kind=jnp.bfloat16):
    level = block_scale(key, shape, shards, -0.22, 0.18) if shards else 1.0
    array = jax.random.normal(key, shape, jnp.float32) * deviation * level
    return jnp.minimum(jnp.maximum(array, -limit), limit).astype(kind)


def setup_inputs(seed: int = 0) -> dict:
    streams_of = jax.random.split(jax.random.key(seed), 6)
    return {
        "sensitivity": centred(streams_of[0], (NW, LAGS, OBS, REG), OBS ** -0.5, 0.1875, ((0, 4), (3, 8))),
        "reach": draw_reach(jax.random.fold_in(streams_of[5], 71), 0),
        "obs_weight": jnp.clip(jnp.exp(math.log(4.0) - 2.7725887 * jax.random.uniform(streams_of[2], (NW, OBS), jnp.float32) ** block_scale(streams_of[2], (NW, OBS), ((0, 4),), -0.2, 0.2)), 0.25, 4.0),
        "prior_precision": jnp.clip(jnp.exp(math.log(4.0) - 2.0794415 * jax.random.uniform(streams_of[3], (NW, REG), jnp.float32) ** block_scale(streams_of[3], (NW, REG), ((0, 4), (1, 8)), -0.2, 0.2)), 0.5, 4.0),
        "pivot_solve": centred(streams_of[4], (REG, REG), REG ** -0.5, 0.09375, ((0, 4), (1, 8))),
    }


def reference(sensitivity, reach, obs_weight, prior_precision, pivot_solve):
    block_rows = []
    for i in range(N_WEEK):
        blocks = []
        for d in range(LAGS):
            total = jnp.zeros((REG, REG), jnp.float32)
            if i - d >= 0:
                for a in range(LAGS - d):
                    w = i + a
                    b = a + d
                    if w < N_WEEK:
                        keep = (reach[w] >= b).astype(jnp.float32) * obs_weight[w]
                        scaled = (keep[:, None] * sensitivity[w, a].astype(jnp.float32)).astype(jnp.bfloat16)
                        total = total + jnp.dot(scaled.T, sensitivity[w, b], preferred_element_type=jnp.float32)
                if d == 0:
                    total = total + jnp.diag(prior_precision[i])
            blocks.append(total)
        block_rows.append(jnp.stack(blocks))
    hessian_band = jnp.stack(block_rows)
    coupling = hessian_band[1, 1].astype(jnp.bfloat16)
    panel = jnp.dot(coupling, pivot_solve.T, preferred_element_type=jnp.float32).astype(jnp.bfloat16)
    schur = hessian_band[1, 0] - jnp.dot(panel, panel.T, preferred_element_type=jnp.float32)
    return hessian_band, panel, schur
```

```python
import functools

import jax
import jax.numpy as jnp
from jax import lax
from jax.experimental import pallas as pl
from jax.experimental.pallas import tpu as pltpu
from jax.sharding import PartitionSpec as P

ROW, COL = "row", "col"


def gather_kernel(n_row, n_col, axis, by_week, x_ref, out_ref, own, ring_s, ring_r, mid_s, mid_r,
                  side_s, side_r, pass_s, pass_r, own_sem):
    row, col = lax.axis_index(ROW), lax.axis_index(COL)
    week = lax.axis_index("week")
    parts, length, width = x_ref.shape
    half = length // 2
    band = (3 * half // 16) // 16 * 16
    up = lax.rem(row + 1, n_row)
    down = lax.rem(row + n_row - 1, n_row)
    ends = ((up, 0), (down, half))
    step_size = width if axis == 2 else length

    barrier = pltpu.get_barrier_semaphore()
    for target in (up, down):
        pl.semaphore_signal(barrier, inc=1, device_id={ROW: target})
    for k in range(1, n_col):
        pl.semaphore_signal(barrier, inc=1, device_id={COL: lax.rem(col + k, n_col)})
    pl.semaphore_wait(barrier, 2 + n_col - 1)

    def place(part, at_row, at_col, first, count):
        start = pl.multiple_of((at_row * n_col + at_col) * step_size, step_size)
        if axis == 2:
            return out_ref.at[part, pl.ds(first, count), pl.ds(start, width)]
        return out_ref.at[part, pl.ds(pl.multiple_of(start + first, 16), count), :]

    def source(part, first, count):
        return x_ref.at[part, pl.ds(first, count), :]

    def origin(step, d):
        return lax.rem(row + (n_row - step if d == 0 else step), n_row)

    def ring(part, step, d, at_col):
        first = ends[d][1]
        at = origin(step, d)
        src = source(part, first, half) if step == 0 else place(part, at, at_col, first, half)
        return pltpu.make_async_remote_copy(
            src, place(part, at, at_col, first, half),
            ring_s.at[part, step, d], ring_r.at[part, step, d], device_id={ROW: ends[d][0]})

    def mid(part, step, d, k):
        first = half - band if d == 0 else half
        at = origin(step, d)
        ref = place(part, at, lax.rem(col + n_col - k, n_col), first, band)
        return pltpu.make_async_remote_copy(
            ref, ref, mid_s.at[part, step, d, k - 1], mid_r.at[part, step, d, k - 1],
            device_id={ROW: ends[d][0]})

    pieces = ((half - band, 2 * band), (0, half - band), (half + band, half - band))

    def side(part, piece, k):
        first, count = pieces[piece]
        return pltpu.make_async_remote_copy(
            source(part, first, count), place(part, row, col, first, count),
            side_s.at[part, piece, k - 1], side_r.at[part, piece, k - 1],
            device_id={COL: lax.rem(col + k, n_col)})

    def onward(part, step, d, k):
        first, count = pieces[1 + d]
        ref = place(part, origin(step, d), col, first, count)
        return pltpu.make_async_remote_copy(
            ref, ref, pass_s.at[part, step - 1, d, k - 1], pass_r.at[part, step - 1, d, k - 1],
            device_id={COL: lax.rem(col + k, n_col)})

    def each(body):
        for part in range(parts):
            if by_week and part > 0:
                pl.when(week >= part)(functools.partial(body, part))
            else:
                body(part)

    peers = range(1, n_col)

    def take_own(part):
        return pltpu.make_async_copy(x_ref.at[part], own.at[part], own_sem.at[part])

    def put_own(part):
        return pltpu.make_async_copy(own.at[part], place(part, row, col, 0, length), own_sem.at[part])

    def begin(part):
        for d in range(2):
            ring(part, 0, d, col).start()
        for k in peers:
            side(part, 0, k).start()
        for k in peers:
            side(part, 1, k).start()
            side(part, 2, k).start()
        take_own(part).start()

    each(begin)

    def spread_mid(part):
        take_own(part).wait()
        put_own(part).start()
        for k in peers:
            side(part, 0, k).wait_recv()
            for d in range(2):
                mid(part, 0, d, k).start()

    each(spread_mid)
    for step in range(1, n_row):
        def advance(part, step=step):
            for d in range(2):
                ring(part, step - 1, d, col).wait_recv()
                if step < n_row - 1:
                    ring(part, step, d, col).start()
                for k in peers:
                    onward(part, step, d, k).start()
                for k in peers:
                    mid(part, step - 1, d, k).wait_recv()
                    if step < n_row - 1:
                        mid(part, step, d, k).start()

        each(advance)

    def finish(part):
        put_own(part).wait()
        for k in peers:
            side(part, 0, k).wait_send()
            side(part, 1, k).wait()
            side(part, 2, k).wait()
        for step in range(n_row - 1):
            for d in range(2):
                ring(part, step, d, col).wait_send()
                for k in peers:
                    mid(part, step, d, k).wait_send()
                    onward(part, step + 1, d, k).wait()

    each(finish)


def gather(x, axis, by_week, collective_id):
    n_row, n_col = lax.axis_size(ROW), lax.axis_size(COL)
    parts, length, width = x.shape
    n = n_row * n_col
    shape = (parts, length, width * n) if axis == 2 else (parts, length * n, width)
    dma = pltpu.SemaphoreType.DMA
    ring_sems = dma((parts, n_row - 1, 2))
    mid_sems = dma((parts, n_row - 1, 2, n_col - 1))
    side_sems = dma((parts, 3, n_col - 1))
    sent = x.size * 2 * (n - 1)
    return pl.pallas_call(
        functools.partial(gather_kernel, n_row, n_col, axis, by_week),
        out_shape=jax.ShapeDtypeStruct(shape, x.dtype),
        in_specs=[pl.BlockSpec(memory_space=pl.ANY)],
        out_specs=pl.BlockSpec(memory_space=pl.ANY),
        scratch_shapes=[
            pltpu.VMEM(x.shape, x.dtype),
            ring_sems, ring_sems, mid_sems, mid_sems, side_sems, side_sems, mid_sems, mid_sems,
            dma((parts,)),
        ],
        compiler_params=pltpu.CompilerParams(collective_id=collective_id, has_side_effects=True),
        cost_estimate=pl.CostEstimate(flops=0, bytes_accessed=sent * 8, transcendentals=0),
    )(x)


def send(block, moves):
    return lax.ppermute(block.astype(jnp.bfloat16), "week", moves)


def contract_first(left, right):
    return lax.dot_general(
        left, right, (((0,), (0,)), ((), ())), preferred_element_type=jnp.float32
    )


def contract_last(left, right):
    return lax.dot_general(
        left, right, (((1,), (1,)), ((), ())), preferred_element_type=jnp.float32
    )


def body(sensitivity, reach, obs_weight, prior_precision, pivot_solve):
    week = lax.axis_index("week")
    n_week, n_row, n_col = (lax.axis_size(name) for name in ("week", ROW, COL))
    local = sensitivity[0]
    slim = local.shape[2]
    regions = slim * n_row * n_col
    full = gather(local, 2, True, 0)

    def product(a, b):
        keep = jnp.where((reach[0] >= b) & (week >= b), obs_weight[0], 0.0)
        left = (keep[:, None] * local[a].astype(jnp.float32)).astype(jnp.bfloat16)
        return jnp.where(week >= b, contract_first(left, full[b]), 0.0)

    down = [(w, w - 1) for w in range(1, n_week)]
    late = [(w, w - 1) for w in range(2, n_week)]
    p11 = product(1, 2).astype(jnp.bfloat16)
    from_later = send(p11, late)
    p01 = product(0, 1)
    from_earlier = send(p01, [(1, 2)])
    h1 = p01 + from_later.astype(jnp.float32)
    mine = jnp.where(
        week == 1, h1, from_earlier.astype(jnp.float32) + p11.astype(jnp.float32)
    ).astype(jnp.bfloat16)
    moves = [[(2, w)] for w in range(3, n_week)]
    moves[0].append((1, 0))
    coupling = jnp.where((week == 1) | (week == 2), mine, 0)
    for move in moves:
        coupling = coupling + send(mine, move)

    p20 = send(product(2, 2), late)
    p10 = send(product(1, 1) + p20.astype(jnp.float32), down)
    first_row = (lax.axis_index(ROW) * n_col + lax.axis_index(COL)) * slim
    row_ids = lax.broadcasted_iota(jnp.int32, (slim, regions), 0)
    col_ids = lax.broadcasted_iota(jnp.int32, (slim, regions), 1)
    diagonal = jnp.where(col_ids == row_ids + first_row, prior_precision[0][:, None], 0.0)
    h0 = product(0, 0) + p10.astype(jnp.float32) + diagonal
    h2 = product(0, 2)
    bands = jnp.stack([h0, h1, h2])

    panel = contract_last(
        coupling, lax.all_gather(pivot_solve, (ROW, COL), axis=1, tiled=True)
    ).astype(jnp.bfloat16)
    gram = contract_last(panel, gather(panel[None], 1, False, 1)[0])
    term = jnp.where(week == 1, h0, 0.0) - gram
    schur = lax.psum_scatter(
        term.astype(jnp.bfloat16), "week", scatter_dimension=1, tiled=True
    ).astype(jnp.float32)
    return (bands[None], panel, schur)


def solution(mesh):
    placed = (
        P("week", None, None, (ROW, COL)),
        P("week", None),
        P("week", None),
        P("week", (ROW, COL)),
        P("week", (ROW, COL)),
    )
    return jax.shard_map(
        body,
        mesh=mesh,
        in_specs=placed,
        out_specs=(
            P("week", None, (ROW, COL), None),
            P((ROW, COL), "week"),
            P((ROW, COL), "week"),
        ),
        check_vma=False,
    )
```
